256 devices in a mesh: depth: 32 (over z, x), tile: 8 (over y, core).
Axes of the slice: x: 4, y: 4, z: 8, core: 2. Of those that a mesh axis runs over, the one named last changes fastest.
Arguments:
- tidal: float32 [32, 3, 131072], P('depth', None, 'tile'), may hold values from -1.5 to 1.5
- plane_weight: float32 [32], P('depth'), may hold values from 0.2 to 1
- plane_step: float32 [32], P('depth'), may hold values from 0.2 to 0.6
- ray_angle: float32 [131072], P('tile'), may hold values from -3.140625 to 3.140625
- dest_tile: int32 [32, 1024, 1], P('depth', 'tile'), may hold values from 0 to 7; in each aligned block of 128 rows (0 to 127, 128 to 255, ..., all dimensions but the last counted through in order) at most 32 rows name the same one
- dest_segment: int32 [32, 1024], P('depth', 'tile'), may hold values from 0 to 255
- interp: bfloat16 [32, 1024, 128, 128], P('depth', 'tile'), may hold values from -0.5 to 0.5
Outputs:
- potential_adjoint: float32 [32, 16, 16384], P('depth', 'tile')
The draws below stay inside these ranges and needn't reach their ends.
Inputs may be any that keep to these rules, and one draw needn't show every extreme that they name: `dest_tile`: in each plane, the 128 blocks of one strip name no strip more than 32 times, a bound that some block reaches.
All inputs are finite; a program needn't handle non-finite values.
Results may differ from the reference program's by a relative error of at most 0.003.
Values sent between devices are 32-bit elements; how exact they have to be, the bound alone decides.
A program may use at most 64 MiB of HBM per device.

```python
import math
import jax
import jax.numpy as jnp
import numpy as np
from jax import lax

BLOCK = 128
COLS = 16384
RBLK = 128
PLANES = 32
NBLK = 1024
RAYS = 131072
CAP = 32
SEGS = 256
NROWS = 16
N_TILE = 8


def with_ends(entries, own_key, low, high):
    place = [jax.random.randint(jax.random.fold_in(own_key, axis), (), 0, length) for axis, length in enumerate(entries.shape)]
    longest = entries.shape.index(max(entries.shape))
    beside = place[:longest] + [(place[longest] + 1) % entries.shape[longest]] + place[longest + 1:]
    return entries.at[tuple(place)].set(low).at[tuple(beside)].set(high)


def level_of(stream_key, extent, shards, low, largest):
    def one(axis_at, blocks):
        draws = jax.random.uniform(jax.random.fold_in(jax.random.fold_in(stream_key, 6), axis_at), (blocks,), jnp.float32, low / len(shards), largest / len(shards))
        return jnp.repeat(jnp.exp(draws), extent[axis_at] // blocks).reshape((-1,) + (1,) * (len(extent) - axis_at - 1))

    loudness = one(*shards[0])
    for cut in shards[1:]:
        loudness = loudness * one(*cut)
    return loudness


def deal_out(stream_key, own, number, rows, number_of, top, bound, slope):
    sequence = jax.random.permutation(stream_key, number_of)
    heavy_load, usual = shares(number_of, rows * top, bound, slope, True), shares(number_of, rows * top, bound, slope, False)
    places = jnp.arange(number_of)

    def named(sizes, offset_by):
        used = int((sizes > 0).sum())
        fixed = max(1, used // 4)
        passed = fixed + (places - fixed + offset_by * (used - fixed)) % max(1, number_of - fixed)
        return jnp.zeros((number_of,), jnp.int32).at[sequence[jnp.where(places < fixed, places, passed)]].set(jnp.asarray(sizes, jnp.int32))

    sizes = jnp.where(number % 4 == 0, named(heavy_load, number // 4), named(usual, number - number // 4 - 1))
    mixed = jax.random.permutation(jax.random.fold_in(own, 3), number_of)
    giver, sink = mixed[0:number_of // 2 * 2:2], mixed[1:number_of // 2 * 2:2]
    room = jnp.minimum(sizes[giver] - 1, bound - sizes[sink]) // 2
    room = jnp.where((giver == sequence[0]) | (sink == sequence[0]) | (sizes[sink] == 0), 0, jnp.maximum(room, 0))
    passed = jax.random.randint(jax.random.fold_in(own, 4), (number_of // 2,), 0, 1 << 20) % (room + 1)
    sizes = sizes.at[giver].add(-passed).at[sink].add(passed)
    members = jnp.searchsorted(jnp.cumsum(sizes), jnp.arange(rows * top), side="right").astype(jnp.int32)
    table = members.reshape(top, rows).T
    table = table[jax.random.permutation(jax.random.fold_in(own, 1), rows)]
    offset_by = jax.random.randint(jax.random.fold_in(own, 2), (rows, 1), 0, top)
    return jnp.take_along_axis(table, (jnp.arange(top)[None, :] + offset_by) % top, axis=1)


def shares(number_of, total, most, slope, full):
    loads = [(1 << 20) // math.isqrt(standing ** slope) + 1 for standing in range(1, number_of + 1)]
    largest = most if full else min(most, max(-(-total // number_of), total * loads[0] // sum(loads)))
    least = 1 if total - largest >= number_of - 1 else 0
    given, surplus = [largest] + [least] * (number_of - 1), total - largest - least * (number_of - 1)
    while surplus > 0:
        candidates = [i for i in range(1, number_of) if given[i] < largest] or [i for i in range(1, number_of) if given[i] < most]
        mass, budget = sum([loads[i] for i in candidates]), surplus
        for i in candidates:
            extra = min(most - given[i], max(1, budget * loads[i] // mass), surplus)
            given[i] = given[i] + extra
            surplus = surplus - extra
    return np.array(given)


def centred(stream_key, dims, width, most, pieces=(), dtype=jnp.bfloat16):
    gain = level_of(stream_key, dims, pieces, -0.22, 0.18) if pieces else 1.0
    result = jax.random.normal(stream_key, dims, jnp.float32) * width * gain
    return jnp.minimum(jnp.maximum(result, -most), most).astype(dtype)


def setup_inputs(seed: int = 0) -> dict:
    key_of = jax.random.split(jax.random.key(seed), 8)
    tidal = centred(key_of[0], (PLANES, 3, RAYS), 0.3, 1.5, ((0, 32), (2, 8)), jnp.float32)
    plane_weight = jnp.clip(0.2 + 0.8 * jax.random.uniform(key_of[1], (PLANES,), jnp.float32) ** level_of(key_of[1], (PLANES,), ((0, 32),), -0.2, 0.2), 0.2, 1.0)
    plane_step = jnp.clip(0.2 + 0.400000021 * jax.random.uniform(key_of[2], (PLANES,), jnp.float32) ** level_of(key_of[2], (PLANES,), ((0, 32),), -0.2, 0.2), 0.2, 0.6)
    ray_angle = jnp.clip(jax.random.uniform(key_of[3], (RAYS,), jnp.float32, -3.140625, 3.140625), -3.140625, 3.140625)
    dest_tile_keys = jax.random.split(jax.random.fold_in(key_of[4], 1), PLANES * NBLK // RBLK)
    dest_tile_turns = jax.random.permutation(jax.random.fold_in(key_of[4], 3), PLANES * NBLK // RBLK)
    dest_tile = jax.vmap(lambda own, number: deal_out(jax.random.fold_in(key_of[4], 2), own, number, RBLK, N_TILE, 1, CAP, 2))(dest_tile_keys, dest_tile_turns).reshape((PLANES, NBLK, 1))
    dest_segment = with_ends(jax.random.randint(key_of[5], (PLANES, NBLK), 0, SEGS), jax.random.fold_in(key_of[5], 1), 0, SEGS - 1).astype(jnp.int32)
    interp = centred(key_of[6], (PLANES, NBLK, BLOCK, BLOCK), BLOCK ** -0.5, 0.5, ((0, 32), (1, 8)))
    return {"tidal": tidal, "plane_weight": plane_weight, "plane_step": plane_step, "ray_angle": ray_angle, "dest_tile": dest_tile, "dest_segment": dest_segment, "interp": interp}


def divergence(ax, ay):
    axp = jnp.pad(ax, ((0, 0), (1, 1)))
    ayp = jnp.pad(ay, ((1, 1), (0, 0)))
    return 0.5 * (axp[:, :-2] - axp[:, 2:]) + 0.5 * (ayp[:-2, :] - ayp[2:, :])


def smooth(raw):
    rp = jnp.pad(raw, ((1, 1), (0, 0)))
    rows_done = 0.25 * rp[:-2, :] + 0.5 * raw + 0.25 * rp[2:, :]
    cp = jnp.pad(rows_done, ((0, 0), (1, 1)))
    return 0.25 * cp[:, :-2] + 0.5 * rows_done + 0.25 * cp[:, 2:]


def reference(tidal, plane_weight, plane_step, ray_angle, dest_tile, dest_segment, interp):
    jxx = tidal[:, 0]
    jxy = tidal[:, 1]
    jyy = tidal[:, 2]
    g_one = -jnp.sum(plane_weight[:, None] * (jxx - jyy) * 0.5, axis=0)
    g_two = -jnp.sum(plane_weight[:, None] * jxy, axis=0)
    cross = -g_one * jnp.sin(2.0 * ray_angle) + g_two * jnp.cos(2.0 * ray_angle)
    xb_one = cross * jnp.cos(ray_angle)
    xb_two = cross * jnp.sin(ray_angle)
    tb_one = jnp.zeros_like(xb_one)
    tb_two = jnp.zeros_like(xb_one)
    adjoints = []
    for plane in range(PLANES - 1, -1, -1):
        step_len = plane_step[plane]
        tp_one = tb_one + step_len * xb_one
        tp_two = tb_two + step_len * xb_two
        adjoints.append(jnp.stack([-tp_one, -tp_two]))
        new_one = xb_one - (jxx[plane] * tp_one + jxy[plane] * tp_two)
        new_two = xb_two - (jxy[plane] * tp_one + jyy[plane] * tp_two)
        xb_one, xb_two = new_one, new_two
        tb_one, tb_two = tp_one, tp_two
    abar = jnp.stack(adjoints[::-1]).astype(jnp.bfloat16)

    def one_plane(inputs):
        plane_abar, plane_dest, plane_seg, plane_interp = inputs
        blocks = jnp.transpose(plane_abar.reshape(2, NBLK, BLOCK), (1, 0, 2))

        def block_group(pair):
            group_abar, group_interp = pair
            return jnp.einsum("bcr,brk->bck", group_abar.astype(jnp.float32), group_interp.astype(jnp.float32))

        groups = NBLK // N_TILE
        contrib = lax.map(block_group, (blocks.reshape(N_TILE, groups, 2, BLOCK), plane_interp.reshape(N_TILE, groups, BLOCK, BLOCK)))
        contrib = contrib.reshape(NBLK, 2, BLOCK)
        target = (plane_dest[:, 0] * SEGS + plane_seg).astype(jnp.int32)
        summed = jnp.zeros((N_TILE * SEGS, 2, BLOCK), jnp.float32).at[target].add(contrib)
        maps = jnp.transpose(summed, (1, 0, 2)).reshape(2, NROWS, COLS)
        return smooth(divergence(maps[0], maps[1]))

    return lax.map(one_plane, (abar, dest_tile, dest_segment, interp))
```

```python
import jax
import jax.numpy as jnp
from jax import lax
from jax.experimental import pallas as pl
from jax.experimental.pallas import tpu as pltpu
from jax.sharding import PartitionSpec as P

ROWS = 2
COLS = 16384
HI = lax.Precision.HIGHEST


def all_to_all(value, axis):
    return lax.all_to_all(value, axis, split_axis=0, concat_axis=0, tiled=True)


def shift_cols(field):
    padded = jnp.pad(field, ((0, 0), (1, 1)))
    return padded[:, :-2], padded[:, 2:]


def sweep_kernel(planes, trig, adjoints):
    count = planes.shape[0]
    g_one = jnp.zeros(planes.shape[2:], jnp.float32)
    g_two = jnp.zeros(planes.shape[2:], jnp.float32)
    for plane in range(count):
        weight = planes[plane, 3, 0:1]
        g_one -= weight * (planes[plane, 0] - planes[plane, 2]) * 0.5
        g_two -= weight * planes[plane, 1]
    cross = -g_one * trig[0] + g_two * trig[1]
    xb_one, xb_two = cross * trig[3], cross * trig[2]
    tb_one = tb_two = jnp.zeros_like(cross)
    for plane in range(count - 1, -1, -1):
        step = planes[plane, 3, 1:2]
        jxx, jxy, jyy = planes[plane, 0], planes[plane, 1], planes[plane, 2]
        tb_one = tb_one + step * xb_one
        tb_two = tb_two + step * xb_two
        adjoints[plane, 0] = -tb_one
        adjoints[plane, 1] = -tb_two
        xb_one, xb_two = (
            xb_one - (jxx * tb_one + jxy * tb_two),
            xb_two - (jxy * tb_one + jyy * tb_two),
        )


def per_device(tidal, plane_weight, plane_step, ray_angle, dest_tile, dest_segment, interp):
    n_tile = lax.axis_size("tile")
    n_depth = lax.axis_size("depth")
    rays = tidal.shape[2]
    part = rays // n_depth
    blocks = interp.shape[1]
    width = interp.shape[2]
    slots = 2 * blocks // n_tile
    segments = ROWS * COLS // width
    here = lax.axis_index("depth")
    tile = lax.axis_index("tile")

    lanes = part // width
    row = lax.broadcasted_iota(jnp.int32, (n_depth, 1, lanes, width), 2)
    scalars = jnp.where(row == 0, plane_weight[0], plane_step[0])
    terms = jnp.transpose(tidal[0].reshape(3, n_depth, lanes, width), (1, 0, 2, 3))
    planes = all_to_all(jnp.concatenate([terms, scalars], axis=1), "depth")
    angle = lax.dynamic_slice(ray_angle, (here * part,), (part,)).reshape(lanes, width)
    trig = jnp.stack(
        [jnp.sin(2.0 * angle), jnp.cos(2.0 * angle), jnp.sin(angle), jnp.cos(angle)]
    )
    adjoints = pl.pallas_call(
        sweep_kernel,
        out_shape=jax.ShapeDtypeStruct((n_depth, 2, lanes, width), jnp.float32),
        in_specs=[pl.BlockSpec(memory_space=pltpu.VMEM)] * 2,
        out_specs=pl.BlockSpec(memory_space=pltpu.VMEM),
    )(planes, trig)
    back = lax.reduce_precision(all_to_all(adjoints, "depth"), 8, 7)
    abar = jnp.transpose(back, (0, 2, 1, 3))
    abar = abar.reshape(blocks, 2, width).astype(jnp.bfloat16)
    contrib = jnp.einsum("bcr,brk->bck", abar, interp[0], preferred_element_type=jnp.float32)

    dest = dest_tile[0, :, 0]
    earlier = jnp.arange(blocks)[None, :] < jnp.arange(blocks)[:, None]
    rank = jnp.sum(jnp.logical_and(dest[:, None] == dest[None, :], earlier), axis=1)
    slot = dest * slots + rank
    pick = (jnp.arange(n_tile * slots)[:, None] == slot[None, :]).astype(jnp.float32)
    send_data = jnp.dot(pick, contrib.reshape(blocks, 2 * width), precision=HI)
    send_ids = jnp.dot(pick, (dest_segment[0] + 1).astype(jnp.float32)[:, None], precision=HI) - 1.0
    got_data = all_to_all(send_data.reshape(n_tile, slots, 2 * width), "tile")
    got_ids = all_to_all(send_ids.astype(jnp.int32).reshape(n_tile, slots), "tile")
    place = (jnp.arange(segments)[:, None] == got_ids.reshape(1, -1)).astype(jnp.float32)
    summed = jnp.dot(place, got_data.reshape(-1, 2 * width), precision=HI)
    ax = summed[:, :width].reshape(ROWS, COLS)
    ay = summed[:, width:].reshape(ROWS, COLS)

    left, right = shift_cols(ax)
    column = 0.5 * (left - right)
    above = jnp.where(tile == 0, 0.0, -0.5 * ay[0])
    below = jnp.where(tile == n_tile - 1, 0.0, 0.5 * ay[1])
    raw_0 = column[0] - 0.5 * ay[1]
    raw_1 = column[1] + 0.5 * ay[0]
    up = jnp.stack([0.25 * above, 0.5 * above + 0.25 * raw_0])
    down = jnp.stack([0.25 * raw_1 + 0.5 * below, 0.25 * below])
    own = jnp.stack(
        [0.25 * above + 0.5 * raw_0 + 0.25 * raw_1, 0.25 * raw_0 + 0.5 * raw_1 + 0.25 * below]
    )
    to_next = [(i, i + 1) for i in range(n_tile - 1)]
    from_next = [(j, i) for i, j in to_next]
    rows_done = own + lax.ppermute(down, "tile", to_next) + lax.ppermute(up, "tile", from_next)
    left, right = shift_cols(rows_done)
    return (0.25 * left + 0.5 * rows_done + 0.25 * right)[None]


def solution(mesh):
    return jax.shard_map(
        per_device,
        mesh=mesh,
        in_specs=(
            P("depth", None, "tile"),
            P("depth"),
            P("depth"),
            P("tile"),
            P("depth", "tile", None),
            P("depth", "tile"),
            P("depth", "tile", None, None),
        ),
        out_specs=P("depth", "tile", None),
        check_vma=False,
    )
```

```python
import jax
import jax.numpy as jnp
from jax import lax
from jax.experimental import pallas as pl
from jax.experimental.pallas import tpu as pltpu
from jax.sharding import PartitionSpec as P

ROWS = 2
WIDTH = 128
X_SIZE = 4
MESH = pl.DeviceIdType.MESH
F32 = jnp.float32
BF16 = jnp.bfloat16


def split_two(value):
    high = value.astype(BF16)
    low = (value - high.astype(F32)).astype(BF16)
    return jnp.concatenate([high, low], axis=1)


def iota(shape, axis):
    return lax.broadcasted_iota(jnp.int32, shape, axis)


def neighbours(field):
    lane, row = iota(field.shape, 1), iota(field.shape, 0)
    rows, lanes = field.shape
    left = pltpu.roll(field, 1, axis=1)
    left = jnp.where(lane == 0, pltpu.roll(left, 1, axis=0), left)
    left = jnp.where(jnp.logical_and(lane == 0, row == 0), 0.0, left)
    right = pltpu.roll(field, lanes - 1, axis=1)
    right = jnp.where(lane == lanes - 1, pltpu.roll(right, rows - 1, axis=0), right)
    right = jnp.where(jnp.logical_and(lane == lanes - 1, row == rows - 1), 0.0, right)
    return left, right


def kernel(
    n_depth, n_tile,
    tidal, angle, interp, dest, segment, weight, step,
    out,
    tid, ang, itp, dst, seg, mine, scalars, planes, adj, back, contrib, pick,
    id_send, id_got, send, got, place, up, down, from_above, from_below,
    local_sem, send_sem, recv_sem,
):
    depth, tile = lax.axis_index("depth"), lax.axis_index("tile")
    blocks = interp.shape[0]
    lanes = blocks // n_depth
    slots = 2 * blocks // n_tile
    columns = 2 * blocks
    segments = place.shape[0]
    rows = segments // ROWS
    n_z, n_x = n_depth // X_SIZE, X_SIZE
    z, x = depth // n_x, depth % n_x
    z_order = sorted(range(n_z), key=lambda dz: -min(dz, n_z - dz))
    x_order = sorted(range(n_x), key=lambda dx: -min(dx, n_x - dx))
    depth_peers = [
        lax.rem(z + dz, n_z) * n_x + lax.rem(x + dx, n_x)
        for dz in z_order for dx in x_order if dz or dx
    ]
    tile_peers = [lax.rem(tile + dt, n_tile) for dt in (3, 5, 4, 2, 6, 1, 7) if dt < n_tile]

    barrier = pltpu.get_barrier_semaphore()
    for peer in depth_peers:
        pl.semaphore_signal(barrier, 1, device_id=(peer, tile), device_id_type=MESH)
    for peer in tile_peers:
        pl.semaphore_signal(barrier, 1, device_id=(depth, peer), device_id_type=MESH)

    loads = [
        pltpu.make_async_copy(source, target, local_sem.at[i])
        for i, (source, target) in enumerate(
            [(tidal, tid), (dest, dst), (segment, seg), (angle, ang), (interp, itp)]
        )
    ]
    for load in loads:
        load.start()
    mine[...] = jnp.where(iota(mine.shape, 0) == 0, weight[0], step[0])
    scalars[depth] = mine[...]
    for load in loads[1:3]:
        load.wait()

    dest_row = jnp.broadcast_to(dst[...], (blocks, blocks)).astype(F32)
    dest_column = dest_row.T
    below_diagonal = iota((blocks, blocks), 0) > iota((blocks, blocks), 1)
    same = (dest_row == dest_column).astype(F32)
    rank_column = jnp.sum(jnp.where(below_diagonal, same, 0.0), axis=1, keepdims=True)
    rank_row = jnp.sum(
        jnp.where(iota((blocks, blocks), 0) < iota((blocks, blocks), 1), same, 0.0),
        axis=0, keepdims=True,
    )
    owner = iota((n_tile, blocks), 0).astype(F32)
    ids = jnp.where(
        jnp.broadcast_to(dst[...], (n_tile, blocks)).astype(F32) == owner,
        jnp.broadcast_to(seg[...], (n_tile, blocks)).astype(F32) + 1.0, 0.0,
    ).astype(BF16)
    at = (rank_column + (tile * slots).astype(F32) == iota((blocks, columns), 1).astype(F32))
    id_rows = jnp.dot(ids, at.astype(F32).astype(BF16), preferred_element_type=F32)
    for t in range(n_tile):
        for h in range(2):
            id_send[t, h:h + 1, :] = id_rows[t:t + 1, h * blocks:(h + 1) * blocks]
    id_got[tile] = id_send[tile]

    slot_row = (dest_row[0:8] * float(slots) + rank_row).astype(BF16)
    q = iota((blocks, columns), 1)
    spread = (iota((blocks, columns), 0) == (q // (2 * lanes)) * lanes + q % lanes)
    slot_q = jnp.dot(slot_row, spread.astype(F32).astype(BF16), preferred_element_type=F32)[0:1]
    q = iota((1, columns), 1)
    key_q = slot_q + ((q // lanes) % 2 * 1024).astype(F32)
    row = iota((2 * n_tile * slots, columns), 0)
    key_row = (row // (2 * slots)) * slots + row % slots + (row // slots) % 2 * 1024
    pick[...] = (key_row.astype(F32) == key_q).astype(F32).astype(BF16)

    loads[0].wait()
    loads[3].wait()
    planes[depth] = tid[:, depth]
    a = ang[depth]
    sin_a, cos_a = jnp.sin(a), jnp.cos(a)
    sin_2a, cos_2a = jnp.sin(2.0 * a), jnp.cos(2.0 * a)

    pl.semaphore_wait(barrier, len(depth_peers) + len(tile_peers))

    def push(source, target, kind, where):
        copy = pltpu.make_async_remote_copy(
            src_ref=source, dst_ref=target, send_sem=send_sem.at[kind], recv_sem=recv_sem.at[kind],
            device_id=where, device_id_type=MESH,
        )
        copy.start()

    def settle(ref, sem):
        pltpu.make_async_copy(ref, ref, sem).wait()

    for peer in depth_peers:
        push(mine, scalars.at[depth], 0, (peer, tile))
        push(tid.at[:, peer], planes.at[depth], 1, (peer, tile))
    for peer in tile_peers:
        push(id_send.at[peer], id_got.at[tile], 2, (depth, peer))

    n_other = n_depth - 1
    settle(scalars.at[pl.ds(0, n_other)], recv_sem.at[0])
    settle(planes.at[pl.ds(0, n_other)], recv_sem.at[1])
    g_one = jnp.zeros((lanes, WIDTH), F32)
    g_two = jnp.zeros((lanes, WIDTH), F32)
    for plane in range(n_depth):
        w = scalars[plane, 0:1]
        g_one -= w * (planes[plane, 0] - planes[plane, 2]) * 0.5
        g_two -= w * planes[plane, 1]
    cross = -g_one * sin_2a + g_two * cos_2a
    xb_one, xb_two = cross * cos_a, cross * sin_a
    tb_one = tb_two = jnp.zeros_like(cross)
    for plane in range(n_depth - 1, -1, -1):
        s = scalars[plane, 1:2]
        jxx, jxy, jyy = planes[plane, 0], planes[plane, 1], planes[plane, 2]
        tb_one = tb_one + s * xb_one
        tb_two = tb_two + s * xb_two
        adj[plane, 0:lanes] = -tb_one
        adj[plane, lanes:2 * lanes] = -tb_two
        xb_one, xb_two = (
            xb_one - (jxx * tb_one + jxy * tb_two),
            xb_two - (jxy * tb_one + jyy * tb_two),
        )
    for peer in depth_peers:
        push(adj.at[peer], back.at[depth], 3, (peer, tile))
    back[depth] = adj[depth]

    settle(id_got.at[pl.ds(0, n_tile - 1)], recv_sem.at[2])
    id_sum = jnp.sum(id_got[...], axis=0) - 1.0
    seg_row = iota((segments, blocks), 0).astype(F32)
    for h in range(2):
        place[:, h * blocks:(h + 1) * blocks] = (
            (seg_row == id_sum[h:h + 1]).astype(F32).astype(BF16)
        )
    loads[4].wait()
    settle(back.at[pl.ds(0, n_other)], recv_sem.at[3])
    part = iota((2 * lanes, WIDTH), 0) % lanes
    for i in range(n_depth):
        value = back[i]
        left = jnp.concatenate([jnp.where(part == j, value, 0.0) for j in range(lanes)], axis=1)
        contrib[2 * lanes * i:2 * lanes * (i + 1), :] = jnp.dot(
            left.astype(BF16), itp[lanes * i:lanes * (i + 1)].reshape(lanes * WIDTH, WIDTH),
            preferred_element_type=F32,
        )
    picked = jnp.dot(pick[...], split_two(contrib[...]), preferred_element_type=F32)
    picked = picked[:, 0:WIDTH] + picked[:, WIDTH:2 * WIDTH]
    send[...] = picked.reshape(send.shape)
    for peer in tile_peers:
        push(send.at[peer], got.at[tile], 4, (depth, peer))
    got[tile] = send[tile]
    settle(got.at[pl.ds(0, n_tile - 1)], recv_sem.at[4])

    both = [
        split_two(got[:, c * slots:(c + 1) * slots, :].reshape(n_tile * slots, WIDTH))
        for c in range(2)
    ]
    ax, ay = [
        total[:, 0:WIDTH] + total[:, WIDTH:2 * WIDTH]
        for total in (jnp.dot(place[...], b, preferred_element_type=F32) for b in both)
    ]
    ay_0, ay_1 = ay[0:rows], ay[rows:]
    above = jnp.where(tile == 0, 0.0, -0.5) * ay_0
    below = jnp.where(tile == n_tile - 1, 0.0, 0.5) * ay_1
    left, right = neighbours(ax[0:rows])
    raw_0 = 0.5 * (left - right) - 0.5 * ay_1
    left, right = neighbours(ax[rows:])
    raw_1 = 0.5 * (left - right) + 0.5 * ay_0
    up[0] = 0.25 * above
    up[1] = 0.5 * above + 0.25 * raw_0
    down[0] = 0.25 * raw_1 + 0.5 * below
    down[1] = 0.25 * below
    before, after = lax.rem(tile + n_tile - 1, n_tile), lax.rem(tile + 1, n_tile)
    push(up, from_below, 5, (depth, before))
    push(down, from_above, 6, (depth, after))
    own = [
        0.25 * above + 0.5 * raw_0 + 0.25 * raw_1,
        0.25 * raw_0 + 0.5 * raw_1 + 0.25 * below,
    ]
    settle(from_below, recv_sem.at[5])
    settle(from_above, recv_sem.at[6])
    has_before = jnp.where(tile == 0, 0.0, 1.0)
    has_after = jnp.where(tile == n_tile - 1, 0.0, 1.0)
    for r in range(ROWS):
        line = own[r] + has_before * from_above[r] + has_after * from_below[r]
        left, right = neighbours(line)
        out[r] = 0.25 * left + 0.5 * line + 0.25 * right

    settle(scalars.at[pl.ds(0, n_other)], send_sem.at[0])
    settle(planes.at[pl.ds(0, n_other)], send_sem.at[1])
    settle(id_got.at[pl.ds(0, n_tile - 1)], send_sem.at[2])
    settle(back.at[pl.ds(0, n_other)], send_sem.at[3])
    settle(got.at[pl.ds(0, n_tile - 1)], send_sem.at[4])
    settle(up, send_sem.at[5])
    settle(down, send_sem.at[6])


def per_device(tidal, plane_weight, plane_step, ray_angle, dest_tile, dest_segment, interp):
    n_tile = lax.axis_size("tile")
    n_depth = lax.axis_size("depth")
    rays = tidal.shape[2]
    blocks = interp.shape[1]
    lanes = blocks // n_depth
    slots = 2 * blocks // n_tile
    segments = 2 * blocks
    rows = segments // ROWS

    def body(*refs):
        kernel(n_depth, n_tile, *refs)

    hbm = pl.BlockSpec(memory_space=pl.ANY)
    smem = pl.BlockSpec(memory_space=pltpu.SMEM)
    vmem = pltpu.VMEM
    out = pl.pallas_call(
        body,
        out_shape=jax.ShapeDtypeStruct((ROWS, rows, WIDTH), F32),
        in_specs=[hbm, hbm, hbm, hbm, hbm, smem, smem],
        out_specs=pl.BlockSpec(memory_space=pltpu.VMEM),
        scratch_shapes=[
            vmem((3, n_depth, lanes, WIDTH), F32),
            vmem((n_depth, lanes, WIDTH), F32),
            vmem((blocks, WIDTH, WIDTH), BF16),
            vmem((1, blocks), jnp.int32),
            vmem((1, blocks), jnp.int32),
            vmem((2, WIDTH), F32),
            vmem((n_depth, 2, WIDTH), F32),
            vmem((n_depth, 3, lanes, WIDTH), F32),
            vmem((n_depth, 2 * lanes, WIDTH), F32),
            vmem((n_depth, 2 * lanes, WIDTH), F32),
            vmem((2 * blocks, WIDTH), F32),
            vmem((2 * n_tile * slots, 2 * blocks), BF16),
            vmem((n_tile, 2, blocks), F32),
            vmem((n_tile, 2, blocks), F32),
            vmem((n_tile, 2 * slots, WIDTH), F32),
            vmem((n_tile, 2 * slots, WIDTH), F32),
            vmem((segments, 2 * blocks), BF16),
            vmem((ROWS, rows, WIDTH), F32),
            vmem((ROWS, rows, WIDTH), F32),
            vmem((ROWS, rows, WIDTH), F32),
            vmem((ROWS, rows, WIDTH), F32),
            pltpu.SemaphoreType.DMA((5,)),
            pltpu.SemaphoreType.DMA((7,)),
            pltpu.SemaphoreType.DMA((7,)),
        ],
        compiler_params=pltpu.CompilerParams(collective_id=0, has_side_effects=True),
    )(
        tidal.reshape(3, n_depth, lanes, WIDTH),
        ray_angle.reshape(n_depth, lanes, WIDTH),
        interp[0],
        dest_tile.reshape(1, blocks),
        dest_segment,
        plane_weight,
        plane_step,
    )
    return out.reshape(1, ROWS, rows * WIDTH)


def solution(mesh):
    return jax.shard_map(
        per_device,
        mesh=mesh,
        in_specs=(
            P("depth", None, "tile"),
            P("depth"),
            P("depth"),
            P("tile"),
            P("depth", "tile", None),
            P("depth", "tile"),
            P("depth", "tile", None, None),
        ),
        out_specs=P("depth", "tile", None),
        check_vma=False,
    )
```

```python
import jax
import jax.numpy as jnp
from jax import lax
from jax.experimental import pallas as pl
from jax.experimental.pallas import tpu as pltpu
from jax.sharding import PartitionSpec as P

ROWS = 2
WIDTH = 128
X_SIZE = 4
MESH = pl.DeviceIdType.MESH
F32 = jnp.float32
BF16 = jnp.bfloat16


def split_two(value):
    high = value.astype(BF16)
    low = (value - high.astype(F32)).astype(BF16)
    return jnp.concatenate([high, low], axis=1)


def iota(shape, axis):
    return lax.broadcasted_iota(jnp.int32, shape, axis)


def neighbours(field):
    lane, row = iota(field.shape, 1), iota(field.shape, 0)
    rows, lanes = field.shape
    left = pltpu.roll(field, 1, axis=1)
    left = jnp.where(lane == 0, pltpu.roll(left, 1, axis=0), left)
    left = jnp.where(jnp.logical_and(lane == 0, row == 0), 0.0, left)
    right = pltpu.roll(field, lanes - 1, axis=1)
    right = jnp.where(lane == lanes - 1, pltpu.roll(right, rows - 1, axis=0), right)
    right = jnp.where(jnp.logical_and(lane == lanes - 1, row == rows - 1), 0.0, right)
    return left, right


def kernel(
    n_depth, n_tile,
    tidal, angle, interp, dest, segment, weight, step,
    out,
    tid, ang, itp, dst, seg, mine, scalars, planes, adj, back, contrib, pick,
    id_send, id_got, send, got, place, up, down, from_above, from_below,
    local_sem, send_sem, recv_sem, back_sem,
):
    depth, tile = lax.axis_index("depth"), lax.axis_index("tile")
    blocks = interp.shape[0]
    lanes = blocks // n_depth
    slots = 2 * blocks // n_tile
    columns = 2 * blocks
    segments = place.shape[0]
    rows = segments // ROWS
    n_z, n_x = n_depth // X_SIZE, X_SIZE
    z, x = depth // n_x, depth % n_x
    z_order = sorted(range(n_z), key=lambda dz: -min(dz, n_z - dz))
    x_order = sorted(range(n_x), key=lambda dx: -min(dx, n_x - dx))
    depth_peers = [
        lax.rem(z + dz, n_z) * n_x + lax.rem(x + dx, n_x)
        for dz in z_order for dx in x_order if dz or dx
    ]
    far_first = sorted(range(n_tile), key=lambda dt: -min(dt, n_tile - dt))
    tile_peers = [lax.rem(tile + dt, n_tile) for dt in far_first[:-1]]

    barrier = pltpu.get_barrier_semaphore()
    for peer in depth_peers:
        pl.semaphore_signal(barrier, 1, device_id=(peer, tile), device_id_type=MESH)
    for peer in tile_peers:
        pl.semaphore_signal(barrier, 1, device_id=(depth, peer), device_id_type=MESH)

    loads = [
        pltpu.make_async_copy(source, target, local_sem.at[i])
        for i, (source, target) in enumerate(
            [(tidal, tid), (dest, dst), (segment, seg), (angle, ang), (interp, itp)]
        )
    ]
    for load in loads:
        load.start()
    for load in loads[1:3]:
        load.wait()
    mine[...] = jnp.where(iota(mine.shape, 1) < WIDTH // 2, weight[0], step[0])
    scalars[depth] = mine[...]

    dest_row = jnp.broadcast_to(dst[...], (blocks, blocks)).astype(F32)
    dest_column = dest_row.T
    below_diagonal = iota((blocks, blocks), 0) > iota((blocks, blocks), 1)
    same = (dest_row == dest_column).astype(F32)
    rank_column = jnp.sum(jnp.where(below_diagonal, same, 0.0), axis=1, keepdims=True)
    rank_row = jnp.sum(
        jnp.where(iota((blocks, blocks), 0) < iota((blocks, blocks), 1), same, 0.0),
        axis=0, keepdims=True,
    )
    owner = iota((n_tile, blocks), 0).astype(F32)
    ids = jnp.where(
        jnp.broadcast_to(dst[...], (n_tile, blocks)).astype(F32) == owner,
        jnp.broadcast_to(seg[...], (n_tile, blocks)).astype(F32) + 1.0, 0.0,
    ).astype(BF16)
    at = (rank_column + (tile * slots).astype(F32) == iota((blocks, columns), 1).astype(F32))
    id_rows = jnp.dot(ids, at.astype(F32).astype(BF16), preferred_element_type=F32)
    for t in range(n_tile):
        for h in range(2):
            id_send[t, h:h + 1, :] = id_rows[t:t + 1, h * blocks:(h + 1) * blocks]
    id_got[tile] = id_send[tile]

    slot_row = (dest_row[0:8] * float(slots) + rank_row).astype(BF16)
    q = iota((blocks, columns), 1)
    spread = (iota((blocks, columns), 0) == (q // (2 * lanes)) * lanes + q % lanes)
    slot_q = jnp.dot(slot_row, spread.astype(F32).astype(BF16), preferred_element_type=F32)[0:1]
    q = iota((1, columns), 1)
    key_q = slot_q + ((q // lanes) % 2 * 1024).astype(F32)
    row = iota((2 * n_tile * slots, 1), 0)
    turn = row // (2 * slots)
    owner_row = tile + sum(jnp.where(turn == k, dt, 0) for k, dt in enumerate(far_first))
    owner_row = jnp.where(owner_row >= n_tile, owner_row - n_tile, owner_row)
    key_row = owner_row * slots + row % slots + (row // slots) % 2 * 1024
    pick[...] = (key_row.astype(F32) == key_q).astype(F32).astype(BF16)

    loads[0].wait()
    loads[3].wait()
    planes[depth] = tid[:, depth]
    a = ang[depth]
    sin_a, cos_a = jnp.sin(a), jnp.cos(a)
    sin_2a, cos_2a = jnp.sin(2.0 * a), jnp.cos(2.0 * a)

    pl.semaphore_wait(barrier, len(depth_peers) + len(tile_peers))

    def push(source, target, kind, where):
        copy = pltpu.make_async_remote_copy(
            src_ref=source, dst_ref=target, send_sem=send_sem.at[kind], recv_sem=recv_sem.at[kind],
            device_id=where, device_id_type=MESH,
        )
        copy.start()

    def settle(ref, sem):
        pltpu.make_async_copy(ref, ref, sem).wait()

    for peer in depth_peers:
        push(mine, scalars.at[depth], 0, (peer, tile))
        push(tid.at[:, peer], planes.at[depth], 1, (peer, tile))
    for peer in tile_peers:
        push(id_send.at[peer], id_got.at[tile], 2, (depth, peer))

    n_other = n_depth - 1
    settle(scalars.at[pl.ds(0, n_other)], recv_sem.at[0])
    settle(planes.at[pl.ds(0, n_other)], recv_sem.at[1])
    g_one = jnp.zeros((lanes, WIDTH), F32)
    g_two = jnp.zeros((lanes, WIDTH), F32)
    for plane in range(n_depth):
        w = jnp.broadcast_to(scalars[plane, :, 0:1], (lanes, WIDTH))
        g_one -= w * (planes[plane, 0] - planes[plane, 2]) * 0.5
        g_two -= w * planes[plane, 1]
    cross = -g_one * sin_2a + g_two * cos_2a
    xb_one, xb_two = cross * cos_a, cross * sin_a
    tb_one = tb_two = jnp.zeros_like(cross)
    for plane in range(n_depth - 1, -1, -1):
        s = jnp.broadcast_to(scalars[plane, :, WIDTH // 2:WIDTH // 2 + 1], (lanes, WIDTH))
        jxx, jxy, jyy = planes[plane, 0], planes[plane, 1], planes[plane, 2]
        tb_one = tb_one + s * xb_one
        tb_two = tb_two + s * xb_two
        adj[plane, 0:lanes] = -tb_one
        adj[plane, lanes:2 * lanes] = -tb_two
        xb_one, xb_two = (
            xb_one - (jxx * tb_one + jxy * tb_two),
            xb_two - (jxy * tb_one + jyy * tb_two),
        )
    for peer, dz, dx in [
        (zt * n_x + lax.rem(x + dx, n_x), zt, dx) for zt in (0, 1, 7, 2, 6, 3, 5, 4) for dx in x_order
    ]:
        copy = pltpu.make_async_remote_copy(
            src_ref=adj.at[peer], dst_ref=back.at[depth], send_sem=send_sem.at[3],
            recv_sem=back_sem.at[z], device_id=(peer, tile), device_id_type=MESH,
        )
        if dx:
            copy.start()
        else:
            pl.when(peer != depth)(copy.start)
    back[depth] = adj[depth]

    settle(id_got.at[pl.ds(0, n_tile - 1)], recv_sem.at[2])
    id_sum = jnp.sum(id_got[...], axis=0) - 1.0
    seg_row = iota((segments, blocks), 0).astype(F32)
    for h in range(2):
        place[:, h * blocks:(h + 1) * blocks] = (
            (seg_row == id_sum[h:h + 1]).astype(F32).astype(BF16)
        )
    loads[4].wait()
    part = iota((2 * lanes, WIDTH), 0) % lanes
    for dz in sorted(range(n_z), key=lambda dz: min(dz, n_z - dz)):
        first = lax.rem(z + dz, n_z) * n_x
        settle(back.at[pl.ds(0, n_x if dz else n_x - 1)], back_sem.at[lax.rem(z + dz, n_z)])
        for dx in range(n_x):
            i = first + dx
            value = back[i]
            left = jnp.concatenate(
                [jnp.where(part == j, value, 0.0) for j in range(lanes)], axis=1
            )
            at_row = pl.multiple_of(2 * lanes * i, 2 * lanes)
            contrib[pl.ds(at_row, 2 * lanes), :] = jnp.dot(
                left.astype(BF16),
                itp[pl.ds(lanes * i, lanes)].reshape(lanes * WIDTH, WIDTH),
                preferred_element_type=F32,
            )
    source = split_two(contrib[...])
    half = n_tile // 2
    for h in range(2):
        picked = jnp.dot(
            pick[h * half * 2 * slots:(h + 1) * half * 2 * slots, :], source,
            preferred_element_type=F32,
        )
        picked = picked[:, 0:WIDTH] + picked[:, WIDTH:2 * WIDTH]
        send[h * half:(h + 1) * half] = picked.reshape(half, 2 * slots, WIDTH)
        for k in range(h * half, min((h + 1) * half, n_tile - 1)):
            push(send.at[k], got.at[tile], 4, (depth, tile_peers[k]))
    got[tile] = send[n_tile - 1]
    settle(got.at[pl.ds(0, n_tile - 1)], recv_sem.at[4])

    both = [
        split_two(got[:, c * slots:(c + 1) * slots, :].reshape(n_tile * slots, WIDTH))
        for c in range(2)
    ]
    ax, ay = [
        total[:, 0:WIDTH] + total[:, WIDTH:2 * WIDTH]
        for total in (jnp.dot(place[...], b, preferred_element_type=F32) for b in both)
    ]
    ay_0, ay_1 = ay[0:rows], ay[rows:]
    above = jnp.where(tile == 0, 0.0, -0.5) * ay_0
    below = jnp.where(tile == n_tile - 1, 0.0, 0.5) * ay_1
    before, after = lax.rem(tile + n_tile - 1, n_tile), lax.rem(tile + 1, n_tile)
    left, right = neighbours(ax[0:rows])
    raw_0 = 0.5 * (left - right) - 0.5 * ay_1
    up[0] = 0.25 * above
    up[1] = 0.5 * above + 0.25 * raw_0
    push(up, from_below, 5, (depth, before))
    left, right = neighbours(ax[rows:])
    raw_1 = 0.5 * (left - right) + 0.5 * ay_0
    down[0] = 0.25 * raw_1 + 0.5 * below
    down[1] = 0.25 * below
    push(down, from_above, 6, (depth, after))
    own = [
        0.25 * above + 0.5 * raw_0 + 0.25 * raw_1,
        0.25 * raw_0 + 0.5 * raw_1 + 0.25 * below,
    ]
    settle(from_below, recv_sem.at[5])
    settle(from_above, recv_sem.at[6])
    has_before = jnp.where(tile == 0, 0.0, 1.0)
    has_after = jnp.where(tile == n_tile - 1, 0.0, 1.0)
    for r in range(ROWS):
        line = own[r] + has_before * from_above[r] + has_after * from_below[r]
        left, right = neighbours(line)
        out[:, r, :] = 0.25 * left + 0.5 * line + 0.25 * right

    settle(scalars.at[pl.ds(0, n_other)], send_sem.at[0])
    settle(planes.at[pl.ds(0, n_other)], send_sem.at[1])
    settle(id_got.at[pl.ds(0, n_tile - 1)], send_sem.at[2])
    settle(back.at[pl.ds(0, n_other)], send_sem.at[3])
    settle(got.at[pl.ds(0, n_tile - 1)], send_sem.at[4])
    settle(up, send_sem.at[5])
    settle(down, send_sem.at[6])


def per_device(tidal, plane_weight, plane_step, ray_angle, dest_tile, dest_segment, interp):
    n_tile = lax.axis_size("tile")
    n_depth = lax.axis_size("depth")
    rays = tidal.shape[2]
    blocks = interp.shape[1]
    lanes = blocks // n_depth
    slots = 2 * blocks // n_tile
    segments = ROWS * rays // WIDTH
    rows = segments // ROWS

    def body(*refs):
        kernel(n_depth, n_tile, *refs)

    hbm = pl.BlockSpec(memory_space=pl.ANY)
    smem = pl.BlockSpec(memory_space=pltpu.SMEM)
    vmem = pltpu.VMEM
    out = pl.pallas_call(
        body,
        out_shape=jax.ShapeDtypeStruct((rows, ROWS, WIDTH), F32),
        in_specs=[hbm, hbm, hbm, hbm, hbm, smem, smem],
        out_specs=pl.BlockSpec(memory_space=pltpu.VMEM),
        scratch_shapes=[
            vmem((3, n_depth, lanes, WIDTH), F32),
            vmem((n_depth, lanes, WIDTH), F32),
            vmem((blocks, WIDTH, WIDTH), BF16),
            vmem((1, blocks), jnp.int32),
            vmem((1, blocks), jnp.int32),
            vmem((1, WIDTH), F32),
            vmem((n_depth, 1, WIDTH), F32),
            vmem((n_depth, 3, lanes, WIDTH), F32),
            vmem((n_depth, 2 * lanes, WIDTH), F32),
            vmem((n_depth, 2 * lanes, WIDTH), F32),
            vmem((2 * blocks, WIDTH), F32),
            vmem((2 * n_tile * slots, 2 * blocks), BF16),
            vmem((n_tile, 2, blocks), F32),
            vmem((n_tile, 2, blocks), F32),
            vmem((n_tile, 2 * slots, WIDTH), F32),
            vmem((n_tile, 2 * slots, WIDTH), F32),
            vmem((segments, 2 * blocks), BF16),
            vmem((ROWS, rows, WIDTH), F32),
            vmem((ROWS, rows, WIDTH), F32),
            vmem((ROWS, rows, WIDTH), F32),
            vmem((ROWS, rows, WIDTH), F32),
            pltpu.SemaphoreType.DMA((5,)),
            pltpu.SemaphoreType.DMA((7,)),
            pltpu.SemaphoreType.DMA((7,)),
            pltpu.SemaphoreType.DMA((n_depth // X_SIZE,)),
        ],
        compiler_params=pltpu.CompilerParams(collective_id=0, vmem_limit_bytes=33554432, has_side_effects=True),
    )(
        pltpu.with_memory_space_constraint(tidal.reshape(3, n_depth, lanes, WIDTH), pltpu.HBM),
        pltpu.with_memory_space_constraint(ray_angle.reshape(n_depth, lanes, WIDTH), pltpu.HBM),
        pltpu.with_memory_space_constraint(interp[0], pltpu.HBM),
        pltpu.with_memory_space_constraint(dest_tile.reshape(1, blocks), pltpu.HBM),
        pltpu.with_memory_space_constraint(dest_segment, pltpu.HBM),
        plane_weight,
        plane_step,
    )
    return out.transpose(1, 0, 2).reshape(1, ROWS, rows * WIDTH)


def solution(mesh):
    return jax.shard_map(
        per_device,
        mesh=mesh,
        in_specs=(
            P("depth", None, "tile"),
            P("depth"),
            P("depth"),
            P("tile"),
            P("depth", "tile", None),
            P("depth", "tile"),
            P("depth", "tile", None, None),
        ),
        out_specs=P("depth", "tile", None),
        check_vma=False,
    )
```

```python
import jax
import jax.numpy as jnp
from jax import lax
from jax.experimental import pallas as pl
from jax.experimental.pallas import tpu as pltpu
from jax.sharding import PartitionSpec as P

ROWS = 2
WIDTH = 128
X_SIZE = 4
MESH = pl.DeviceIdType.MESH
F32 = jnp.float32
BF16 = jnp.bfloat16


def split_two(value):
    high = value.astype(BF16)
    low = (value - high.astype(F32)).astype(BF16)
    return jnp.concatenate([high, low], axis=1)


def iota(shape, axis):
    return lax.broadcasted_iota(jnp.int32, shape, axis)


def neighbours(field):
    lane, row = iota(field.shape, 1), iota(field.shape, 0)
    rows, lanes = field.shape
    left = pltpu.roll(field, 1, axis=1)
    left = jnp.where(lane == 0, pltpu.roll(left, 1, axis=0), left)
    left = jnp.where(jnp.logical_and(lane == 0, row == 0), 0.0, left)
    right = pltpu.roll(field, lanes - 1, axis=1)
    right = jnp.where(lane == lanes - 1, pltpu.roll(right, rows - 1, axis=0), right)
    right = jnp.where(jnp.logical_and(lane == lanes - 1, row == rows - 1), 0.0, right)
    return left, right


def smooth(line):
    left, right = neighbours(line)
    return 0.25 * left + 0.5 * line + 0.25 * right


def kernel(
    n_depth, n_tile,
    tidal, angle, interp, dest, segment, weight, step,
    out,
    tid, ang, itp, dst, seg, mine, scalars, planes, adj, back, contrib, pick,
    id_send, id_got, send, got, place, up, down, from_above, from_below,
    local_sem, send_sem, recv_sem, back_sem,
):
    depth, tile = lax.axis_index("depth"), lax.axis_index("tile")
    blocks = interp.shape[0]
    lanes = blocks // n_depth
    slots = 2 * blocks // n_tile
    columns = 2 * blocks
    segments = place.shape[0]
    rows = segments // ROWS
    n_z, n_x = n_depth // X_SIZE, X_SIZE
    z, x = depth // n_x, depth % n_x
    z_order = sorted(range(n_z), key=lambda dz: -min(dz, n_z - dz))
    x_order = sorted(range(n_x), key=lambda dx: -min(dx, n_x - dx))
    depth_peers = [
        lax.rem(z + dz, n_z) * n_x + lax.rem(x + dx, n_x)
        for dz in z_order for dx in x_order if dz or dx
    ]
    far_first = sorted(range(n_tile), key=lambda dt: -min(dt, n_tile - dt))
    tile_peers = [lax.rem(tile + dt, n_tile) for dt in far_first[:-1]]

    barrier = pltpu.get_barrier_semaphore()
    for peer in depth_peers:
        pl.semaphore_signal(barrier, 1, device_id=(peer, tile), device_id_type=MESH)
    for peer in tile_peers:
        pl.semaphore_signal(barrier, 1, device_id=(depth, peer), device_id_type=MESH)

    loads = [
        pltpu.make_async_copy(source, target, local_sem.at[i])
        for i, (source, target) in enumerate(
            [(tidal, tid), (dest, dst), (segment, seg), (angle, ang), (interp, itp)]
        )
    ]
    for load in loads:
        load.start()
    for load in loads[1:3]:
        load.wait()
    mine[...] = jnp.where(iota(mine.shape, 1) < WIDTH // 2, weight[0], step[0])
    scalars[depth] = mine[...]

    dest_row = jnp.broadcast_to(dst[...], (blocks, blocks)).astype(F32)
    dest_column = dest_row.T
    below_diagonal = iota((blocks, blocks), 0) > iota((blocks, blocks), 1)
    same = (dest_row == dest_column).astype(F32)
    rank_column = jnp.sum(jnp.where(below_diagonal, same, 0.0), axis=1, keepdims=True)
    rank_row = jnp.sum(
        jnp.where(iota((blocks, blocks), 0) < iota((blocks, blocks), 1), same, 0.0),
        axis=0, keepdims=True,
    )
    owner = iota((n_tile, blocks), 0).astype(F32)
    ids = jnp.where(
        jnp.broadcast_to(dst[...], (n_tile, blocks)).astype(F32) == owner,
        jnp.broadcast_to(seg[...], (n_tile, blocks)).astype(F32) + 1.0, 0.0,
    ).astype(BF16)
    at = (rank_column + (tile * slots).astype(F32) == iota((blocks, columns), 1).astype(F32))
    id_rows = jnp.dot(ids, at.astype(F32).astype(BF16), preferred_element_type=F32)
    for t in range(n_tile):
        for h in range(2):
            id_send[t, h:h + 1, :] = id_rows[t:t + 1, h * blocks:(h + 1) * blocks]
    id_got[tile] = id_send[tile]

    slot_row = (dest_row[0:8] * float(slots) + rank_row).astype(BF16)
    q = iota((blocks, columns), 1)
    spread = (iota((blocks, columns), 0) == (q // (2 * lanes)) * lanes + q % lanes)
    slot_q = jnp.dot(slot_row, spread.astype(F32).astype(BF16), preferred_element_type=F32)[0:1]
    q = iota((1, columns), 1)
    key_q = slot_q + ((q // lanes) % 2 * 1024).astype(F32)
    row = iota((2 * n_tile * slots, 1), 0)
    turn = row // slots % n_tile
    owner_row = tile + sum(jnp.where(turn == k, dt, 0) for k, dt in enumerate(far_first))
    owner_row = jnp.where(owner_row >= n_tile, owner_row - n_tile, owner_row)
    y_first = jnp.where(row < n_tile * slots, 1024, 0)
    key_row = owner_row * slots + row % slots + y_first
    pick[...] = (key_row.astype(F32) == key_q).astype(F32).astype(BF16)

    loads[0].wait()
    loads[3].wait()
    planes[depth] = tid[:, depth]
    a = ang[depth]
    sin_a, cos_a = jnp.sin(a), jnp.cos(a)
    sin_2a, cos_2a = jnp.sin(2.0 * a), jnp.cos(2.0 * a)

    pl.semaphore_wait(barrier, len(depth_peers) + len(tile_peers))

    def push(source, target, kind, where):
        copy = pltpu.make_async_remote_copy(
            src_ref=source, dst_ref=target, send_sem=send_sem.at[kind], recv_sem=recv_sem.at[kind],
            device_id=where, device_id_type=MESH,
        )
        copy.start()

    def settle(ref, sem):
        pltpu.make_async_copy(ref, ref, sem).wait()

    for peer in depth_peers:
        push(mine, scalars.at[depth], 0, (peer, tile))
        push(tid.at[:, peer], planes.at[depth], 1, (peer, tile))
    for peer in tile_peers:
        push(id_send.at[peer], id_got.at[tile], 2, (depth, peer))

    n_other = n_depth - 1
    settle(scalars.at[pl.ds(0, n_other)], recv_sem.at[0])
    settle(planes.at[pl.ds(0, n_other)], recv_sem.at[1])
    g_one = jnp.zeros((lanes, WIDTH), F32)
    g_two = jnp.zeros((lanes, WIDTH), F32)
    for plane in range(n_depth):
        w = jnp.broadcast_to(scalars[plane, :, 0:1], (lanes, WIDTH))
        g_one -= w * (planes[plane, 0] - planes[plane, 2]) * 0.5
        g_two -= w * planes[plane, 1]
    cross = -g_one * sin_2a + g_two * cos_2a
    xb_one, xb_two = cross * cos_a, cross * sin_a
    tb_one = tb_two = jnp.zeros_like(cross)
    for plane in range(n_depth - 1, -1, -1):
        s = jnp.broadcast_to(scalars[plane, :, WIDTH // 2:WIDTH // 2 + 1], (lanes, WIDTH))
        jxx, jxy, jyy = planes[plane, 0], planes[plane, 1], planes[plane, 2]
        tb_one = tb_one + s * xb_one
        tb_two = tb_two + s * xb_two
        adj[plane, 0:lanes] = -tb_one
        adj[plane, lanes:2 * lanes] = -tb_two
        xb_one, xb_two = (
            xb_one - (jxx * tb_one + jxy * tb_two),
            xb_two - (jxy * tb_one + jyy * tb_two),
        )
    for peer in [zt * n_x + xt for zt in (0, 1, 7, 2, 6, 3, 5, 4) for xt in (0, 1, 3, 2)]:
        copy = pltpu.make_async_remote_copy(
            src_ref=adj.at[peer], dst_ref=back.at[depth], send_sem=send_sem.at[3],
            recv_sem=back_sem.at[z], device_id=(peer, tile), device_id_type=MESH,
        )
        pl.when(peer != depth)(copy.start)
    back[depth] = adj[depth]

    settle(id_got.at[pl.ds(0, n_tile - 1)], recv_sem.at[2])
    id_sum = jnp.sum(id_got[...], axis=0) - 1.0
    seg_row = iota((segments, blocks), 0).astype(F32)
    for h in range(2):
        place[:, h * blocks:(h + 1) * blocks] = (
            (seg_row == id_sum[h:h + 1]).astype(F32).astype(BF16)
        )
    loads[4].wait()
    part = iota((2 * lanes, WIDTH), 0) % lanes
    for dz in sorted(range(n_z), key=lambda dz: min(dz, n_z - dz)):
        first = lax.rem(z + dz, n_z) * n_x
        settle(back.at[pl.ds(0, n_x if dz else n_x - 1)], back_sem.at[lax.rem(z + dz, n_z)])
        for dx in range(n_x):
            i = first + dx
            value = back[i]
            left = jnp.concatenate(
                [jnp.where(part == j, value, 0.0) for j in range(lanes)], axis=1
            )
            at_row = pl.multiple_of(2 * lanes * i, 2 * lanes)
            contrib[pl.ds(at_row, 2 * lanes), :] = jnp.dot(
                left.astype(BF16),
                itp[pl.ds(lanes * i, lanes)].reshape(lanes * WIDTH, WIDTH),
                preferred_element_type=F32,
            )
    source = split_two(contrib[...])
    for h in range(2):
        picked = jnp.dot(
            pick[h * n_tile * slots:(h + 1) * n_tile * slots, :], source,
            preferred_element_type=F32,
        )
        picked = picked[:, 0:WIDTH] + picked[:, WIDTH:2 * WIDTH]
        send[h] = picked.reshape(n_tile, slots, WIDTH)
        for k, peer in enumerate(tile_peers):
            push(send.at[h, k], got.at[h, tile], 4 + h, (depth, peer))
        got[h, tile] = send[h, n_tile - 1]

    def arrived(h):
        settle(got.at[h, pl.ds(0, n_tile - 1)], recv_sem.at[4 + h])
        total = jnp.dot(
            place[...], split_two(got[h].reshape(n_tile * slots, WIDTH)),
            preferred_element_type=F32,
        )
        total = total[:, 0:WIDTH] + total[:, WIDTH:2 * WIDTH]
        return total[0:rows], total[rows:]

    before, after = lax.rem(tile + n_tile - 1, n_tile), lax.rem(tile + 1, n_tile)
    ay_0, ay_1 = arrived(0)
    above = jnp.where(tile == 0, 0.0, -0.5) * ay_0
    below = jnp.where(tile == n_tile - 1, 0.0, 0.5) * ay_1
    up[0] = smooth(0.25 * above)
    down[1] = smooth(0.25 * below)
    push(up.at[0], from_below.at[0], 6, (depth, before))
    push(down.at[1], from_above.at[1], 7, (depth, after))
    ax_0, ax_1 = arrived(1)
    left, right = neighbours(ax_0)
    raw_0 = 0.5 * (left - right) - 0.5 * ay_1
    up[1] = smooth(0.5 * above + 0.25 * raw_0)
    push(up.at[1], from_below.at[1], 8, (depth, before))
    left, right = neighbours(ax_1)
    raw_1 = 0.5 * (left - right) + 0.5 * ay_0
    down[0] = smooth(0.25 * raw_1 + 0.5 * below)
    push(down.at[0], from_above.at[0], 9, (depth, after))
    own = [
        smooth(0.25 * above + 0.5 * raw_0 + 0.25 * raw_1),
        smooth(0.25 * raw_0 + 0.5 * raw_1 + 0.25 * below),
    ]
    for kind, ref in enumerate(
        [from_below.at[0], from_above.at[1], from_below.at[1], from_above.at[0]], 6
    ):
        settle(ref, recv_sem.at[kind])
    has_before = jnp.where(tile == 0, 0.0, 1.0)
    has_after = jnp.where(tile == n_tile - 1, 0.0, 1.0)
    for r in range(ROWS):
        out[:, r, :] = own[r] + has_before * from_above[r] + has_after * from_below[r]

    settle(scalars.at[pl.ds(0, n_other)], send_sem.at[0])
    settle(planes.at[pl.ds(0, n_other)], send_sem.at[1])
    settle(id_got.at[pl.ds(0, n_tile - 1)], send_sem.at[2])
    settle(back.at[pl.ds(0, n_other)], send_sem.at[3])
    for h in range(2):
        settle(got.at[h, pl.ds(0, n_tile - 1)], send_sem.at[4 + h])
    for kind, ref in enumerate([up.at[0], down.at[1], up.at[1], down.at[0]], 6):
        settle(ref, send_sem.at[kind])


def per_device(tidal, plane_weight, plane_step, ray_angle, dest_tile, dest_segment, interp):
    n_tile = lax.axis_size("tile")
    n_depth = lax.axis_size("depth")
    rays = tidal.shape[2]
    blocks = interp.shape[1]
    lanes = blocks // n_depth
    slots = 2 * blocks // n_tile
    segments = ROWS * rays // WIDTH
    rows = segments // ROWS

    def body(*refs):
        kernel(n_depth, n_tile, *refs)

    hbm = pl.BlockSpec(memory_space=pl.ANY)
    smem = pl.BlockSpec(memory_space=pltpu.SMEM)
    vmem = pltpu.VMEM
    out = pl.pallas_call(
        body,
        out_shape=jax.ShapeDtypeStruct((rows, ROWS, WIDTH), F32),
        in_specs=[hbm, hbm, hbm, hbm, hbm, smem, smem],
        out_specs=pl.BlockSpec(memory_space=pltpu.VMEM),
        scratch_shapes=[
            vmem((3, n_depth, lanes, WIDTH), F32),
            vmem((n_depth, lanes, WIDTH), F32),
            vmem((blocks, WIDTH, WIDTH), BF16),
            vmem((1, blocks), jnp.int32),
            vmem((1, blocks), jnp.int32),
            vmem((1, WIDTH), F32),
            vmem((n_depth, 1, WIDTH), F32),
            vmem((n_depth, 3, lanes, WIDTH), F32),
            vmem((n_depth, 2 * lanes, WIDTH), F32),
            vmem((n_depth, 2 * lanes, WIDTH), F32),
            vmem((2 * blocks, WIDTH), F32),
            vmem((2 * n_tile * slots, 2 * blocks), BF16),
            vmem((n_tile, 2, blocks), F32),
            vmem((n_tile, 2, blocks), F32),
            vmem((2, n_tile, slots, WIDTH), F32),
            vmem((2, n_tile, slots, WIDTH), F32),
            vmem((segments, 2 * blocks), BF16),
            vmem((ROWS, rows, WIDTH), F32),
            vmem((ROWS, rows, WIDTH), F32),
            vmem((ROWS, rows, WIDTH), F32),
            vmem((ROWS, rows, WIDTH), F32),
            pltpu.SemaphoreType.DMA((5,)),
            pltpu.SemaphoreType.DMA((10,)),
            pltpu.SemaphoreType.DMA((10,)),
            pltpu.SemaphoreType.DMA((n_depth // X_SIZE,)),
        ],
        compiler_params=pltpu.CompilerParams(collective_id=0, vmem_limit_bytes=33554432, has_side_effects=True),
    )(
        pltpu.with_memory_space_constraint(tidal.reshape(3, n_depth, lanes, WIDTH), pltpu.HBM),
        pltpu.with_memory_space_constraint(ray_angle.reshape(n_depth, lanes, WIDTH), pltpu.HBM),
        pltpu.with_memory_space_constraint(interp[0], pltpu.HBM),
        pltpu.with_memory_space_constraint(dest_tile.reshape(1, blocks), pltpu.HBM),
        pltpu.with_memory_space_constraint(dest_segment, pltpu.HBM),
        plane_weight,
        plane_step,
    )
    return out.transpose(1, 0, 2).reshape(1, ROWS, rows * WIDTH)


def solution(mesh):
    return jax.shard_map(
        per_device,
        mesh=mesh,
        in_specs=(
            P("depth", None, "tile"),
            P("depth"),
            P("depth"),
            P("tile"),
            P("depth", "tile", None),
            P("depth", "tile"),
            P("depth", "tile", None, None),
        ),
        out_specs=P("depth", "tile", None),
        check_vma=False,
    )
```

```python
import jax
import jax.numpy as jnp
from jax import lax
from jax.experimental import pallas as pl
from jax.experimental.pallas import tpu as pltpu
from jax.sharding import PartitionSpec as P

ROWS = 2
WIDTH = 128
X_SIZE = 4
MESH = pl.DeviceIdType.MESH
F32 = jnp.float32
BF16 = jnp.bfloat16


def split_two(value):
    high = value.astype(BF16)
    low = (value - high.astype(F32)).astype(BF16)
    return jnp.concatenate([high, low], axis=1)


def iota(shape, axis):
    return lax.broadcasted_iota(jnp.int32, shape, axis)


def neighbours(field):
    lane, row = iota(field.shape, 1), iota(field.shape, 0)
    rows, lanes = field.shape
    left = pltpu.roll(field, 1, axis=1)
    left = jnp.where(lane == 0, pltpu.roll(left, 1, axis=0), left)
    left = jnp.where(jnp.logical_and(lane == 0, row == 0), 0.0, left)
    right = pltpu.roll(field, lanes - 1, axis=1)
    right = jnp.where(lane == lanes - 1, pltpu.roll(right, rows - 1, axis=0), right)
    right = jnp.where(jnp.logical_and(lane == lanes - 1, row == rows - 1), 0.0, right)
    return left, right


def smooth(line):
    left, right = neighbours(line)
    return 0.25 * left + 0.5 * line + 0.25 * right


def kernel(
    n_depth, n_tile,
    tidal, angle, interp, dest, segment, weight, step,
    out,
    tid, ang, itp, dst, seg, mine, scalars, planes, adj, back, contrib, pick,
    id_send, id_got, send, got, place, up, down, from_above, from_below,
    local_sem, send_sem, recv_sem, back_sem,
):
    depth, tile = lax.axis_index("depth"), lax.axis_index("tile")
    blocks = interp.shape[0]
    lanes = blocks // n_depth
    slots = 2 * blocks // n_tile
    columns = 2 * blocks
    segments = place.shape[0]
    rows = segments // ROWS
    n_z, n_x = n_depth // X_SIZE, X_SIZE
    z, x = depth // n_x, depth % n_x
    z_order = sorted(range(n_z), key=lambda dz: -min(dz, n_z - dz))
    x_order = sorted(range(n_x), key=lambda dx: -min(dx, n_x - dx))
    depth_peers = [
        lax.rem(z + dz, n_z) * n_x + lax.rem(x + dx, n_x)
        for dz in z_order for dx in x_order if dz or dx
    ]
    far_first = sorted(range(n_tile), key=lambda dt: -min(dt, n_tile - dt))
    tile_peers = [lax.rem(tile + dt, n_tile) for dt in far_first[:-1]]

    barrier = pltpu.get_barrier_semaphore()
    for peer in depth_peers:
        pl.semaphore_signal(barrier, 1, device_id=(peer, tile), device_id_type=MESH)
    for peer in tile_peers:
        pl.semaphore_signal(barrier, 1, device_id=(depth, peer), device_id_type=MESH)

    loads = [
        pltpu.make_async_copy(source, target, local_sem.at[i])
        for i, (source, target) in enumerate(
            [(tidal, tid), (dest, dst), (segment, seg), (angle, ang), (interp, itp)]
        )
    ]
    for load in loads:
        load.start()
    for load in loads[1:3]:
        load.wait()
    mine[...] = jnp.where(iota(mine.shape, 1) < WIDTH // 2, weight[0], step[0])
    scalars[depth] = mine[...]

    dest_row = jnp.broadcast_to(dst[...], (blocks, blocks)).astype(F32)
    dest_column = dest_row.T
    below_diagonal = iota((blocks, blocks), 0) > iota((blocks, blocks), 1)
    same = (dest_row == dest_column).astype(F32)
    rank_column = jnp.sum(jnp.where(below_diagonal, same, 0.0), axis=1, keepdims=True)
    rank_row = jnp.sum(
        jnp.where(iota((blocks, blocks), 0) < iota((blocks, blocks), 1), same, 0.0),
        axis=0, keepdims=True,
    )
    owner = iota((n_tile, blocks), 0).astype(F32)
    ids = jnp.where(
        jnp.broadcast_to(dst[...], (n_tile, blocks)).astype(F32) == owner,
        jnp.broadcast_to(seg[...], (n_tile, blocks)).astype(F32) + 1.0, 0.0,
    ).astype(BF16)
    at = (rank_column + (tile * slots).astype(F32) == iota((blocks, columns), 1).astype(F32))
    id_rows = jnp.dot(ids, at.astype(F32).astype(BF16), preferred_element_type=F32)
    for t in range(n_tile):
        for h in range(2):
            id_send[t, h:h + 1, :] = id_rows[t:t + 1, h * blocks:(h + 1) * blocks]
    id_got[tile] = id_send[tile]

    slot_row = (dest_row[0:8] * float(slots) + rank_row).astype(BF16)
    q = iota((blocks, columns), 1)
    spread = (iota((blocks, columns), 0) == (q // (2 * lanes)) * lanes + q % lanes)
    slot_q = jnp.dot(slot_row, spread.astype(F32).astype(BF16), preferred_element_type=F32)[0:1]
    q = iota((1, columns), 1)
    key_q = slot_q + ((q // lanes) % 2 * 1024).astype(F32)
    row = iota((2 * n_tile * slots, 1), 0)
    turn = row // slots % n_tile
    owner_row = tile + sum(jnp.where(turn == k, dt, 0) for k, dt in enumerate(far_first))
    owner_row = jnp.where(owner_row >= n_tile, owner_row - n_tile, owner_row)
    y_first = jnp.where(row < n_tile * slots, 1024, 0)
    key_row = owner_row * slots + row % slots + y_first
    pick[...] = (key_row.astype(F32) == key_q).astype(F32).astype(BF16)

    loads[0].wait()
    loads[3].wait()
    planes[depth] = tid[:, depth]
    a = ang[depth]
    sin_a, cos_a = jnp.sin(a), jnp.cos(a)
    sin_2a, cos_2a = jnp.sin(2.0 * a), jnp.cos(2.0 * a)

    pl.semaphore_wait(barrier, len(depth_peers) + len(tile_peers))

    def push(source, target, kind, where):
        copy = pltpu.make_async_remote_copy(
            src_ref=source, dst_ref=target, send_sem=send_sem.at[kind], recv_sem=recv_sem.at[kind],
            device_id=where, device_id_type=MESH,
        )
        copy.start()

    def settle(ref, sem):
        pltpu.make_async_copy(ref, ref, sem).wait()

    for peer in depth_peers:
        push(mine, scalars.at[depth], 0, (peer, tile))
        push(tid.at[:, peer], planes.at[depth], 1, (peer, tile))
    for peer in tile_peers:
        push(id_send.at[peer], id_got.at[tile], 2, (depth, peer))

    n_other = n_depth - 1
    settle(scalars.at[pl.ds(0, n_other)], recv_sem.at[0])
    settle(planes.at[pl.ds(0, n_other)], recv_sem.at[1])
    g_one = jnp.zeros((lanes, WIDTH), F32)
    g_two = jnp.zeros((lanes, WIDTH), F32)
    for plane in range(n_depth):
        w = jnp.broadcast_to(scalars[plane, :, 0:1], (lanes, WIDTH))
        g_one -= w * (planes[plane, 0] - planes[plane, 2]) * 0.5
        g_two -= w * planes[plane, 1]
    cross = -g_one * sin_2a + g_two * cos_2a
    xb_one, xb_two = cross * cos_a, cross * sin_a
    tb_one = tb_two = jnp.zeros_like(cross)
    for plane in range(n_depth - 1, -1, -1):
        s = jnp.broadcast_to(scalars[plane, :, WIDTH // 2:WIDTH // 2 + 1], (lanes, WIDTH))
        jxx, jxy, jyy = planes[plane, 0], planes[plane, 1], planes[plane, 2]
        cross_term = s * jxy
        keep_one, keep_two = 1.0 - s * jxx, 1.0 - s * jyy
        next_one = keep_one * xb_one - cross_term * xb_two - (jxx * tb_one + jxy * tb_two)
        next_two = keep_two * xb_two - cross_term * xb_one - (jxy * tb_one + jyy * tb_two)
        tb_one = tb_one + s * xb_one
        tb_two = tb_two + s * xb_two
        adj[plane, 0:lanes] = -tb_one
        adj[plane, lanes:2 * lanes] = -tb_two
        xb_one, xb_two = next_one, next_two
    for peer in [zt * n_x + xt for zt in (0, 1, 7, 2, 6, 3, 5, 4) for xt in (0, 1, 3, 2)]:
        copy = pltpu.make_async_remote_copy(
            src_ref=adj.at[peer], dst_ref=back.at[depth], send_sem=send_sem.at[3],
            recv_sem=back_sem.at[z], device_id=(peer, tile), device_id_type=MESH,
        )
        pl.when(peer != depth)(copy.start)
    back[depth] = adj[depth]

    settle(id_got.at[pl.ds(0, n_tile - 1)], recv_sem.at[2])
    id_sum = jnp.sum(id_got[...], axis=0) - 1.0
    seg_row = iota((segments, blocks), 0).astype(F32)
    for h in range(2):
        place[:, h * blocks:(h + 1) * blocks] = (
            (seg_row == id_sum[h:h + 1]).astype(F32).astype(BF16)
        )
    loads[4].wait()
    part = iota((2 * lanes, WIDTH), 0) % lanes
    for dz in sorted(range(n_z), key=lambda dz: min(dz, n_z - dz)):
        first = lax.rem(z + dz, n_z) * n_x
        settle(back.at[pl.ds(0, n_x if dz else n_x - 1)], back_sem.at[lax.rem(z + dz, n_z)])
        for dx in range(n_x):
            i = first + dx
            value = back[i]
            left = jnp.concatenate(
                [jnp.where(part == j, value, 0.0) for j in range(lanes)], axis=1
            )
            at_row = pl.multiple_of(2 * lanes * i, 2 * lanes)
            contrib[pl.ds(at_row, 2 * lanes), :] = jnp.dot(
                left.astype(BF16),
                itp[pl.ds(lanes * i, lanes)].reshape(lanes * WIDTH, WIDTH),
                preferred_element_type=F32,
            )
    source = split_two(contrib[...])
    for h in range(2):
        picked = jnp.dot(
            pick[h * n_tile * slots:(h + 1) * n_tile * slots, :], source,
            preferred_element_type=F32,
        )
        picked = picked[:, 0:WIDTH] + picked[:, WIDTH:2 * WIDTH]
        send[h] = picked.reshape(n_tile, slots, WIDTH)
        for k, peer in enumerate(tile_peers):
            push(send.at[h, k], got.at[h, tile], 4 + h, (depth, peer))
        got[h, tile] = send[h, n_tile - 1]

    def arrived(h):
        settle(got.at[h, pl.ds(0, n_tile - 1)], recv_sem.at[4 + h])
        total = jnp.dot(
            place[...], split_two(got[h].reshape(n_tile * slots, WIDTH)),
            preferred_element_type=F32,
        )
        total = total[:, 0:WIDTH] + total[:, WIDTH:2 * WIDTH]
        return total[0:rows], total[rows:]

    before, after = lax.rem(tile + n_tile - 1, n_tile), lax.rem(tile + 1, n_tile)
    ay_0, ay_1 = arrived(0)
    above = jnp.where(tile == 0, 0.0, -0.5) * ay_0
    below = jnp.where(tile == n_tile - 1, 0.0, 0.5) * ay_1
    up[0] = smooth(0.25 * above)
    down[1] = smooth(0.25 * below)
    push(down.at[1], from_above.at[1], 7, (depth, after))
    push(up.at[0], from_below.at[0], 6, (depth, before))
    ax_0, ax_1 = arrived(1)
    left, right = neighbours(ax_0)
    raw_0 = 0.5 * (left - right) - 0.5 * ay_1
    up[1] = smooth(0.5 * above + 0.25 * raw_0)
    push(up.at[1], from_below.at[1], 8, (depth, before))
    left, right = neighbours(ax_1)
    raw_1 = 0.5 * (left - right) + 0.5 * ay_0
    down[0] = smooth(0.25 * raw_1 + 0.5 * below)
    push(down.at[0], from_above.at[0], 9, (depth, after))
    own = [
        smooth(0.25 * above + 0.5 * raw_0 + 0.25 * raw_1),
        smooth(0.25 * raw_0 + 0.5 * raw_1 + 0.25 * below),
    ]
    for kind, ref in enumerate(
        [from_below.at[0], from_above.at[1], from_below.at[1], from_above.at[0]], 6
    ):
        settle(ref, recv_sem.at[kind])
    has_before = jnp.where(tile == 0, 0.0, 1.0)
    has_after = jnp.where(tile == n_tile - 1, 0.0, 1.0)
    for r in range(ROWS):
        out[:, r, :] = own[r] + has_before * from_above[r] + has_after * from_below[r]

    settle(scalars.at[pl.ds(0, n_other)], send_sem.at[0])
    settle(planes.at[pl.ds(0, n_other)], send_sem.at[1])
    settle(id_got.at[pl.ds(0, n_tile - 1)], send_sem.at[2])
    settle(back.at[pl.ds(0, n_other)], send_sem.at[3])
    for h in range(2):
        settle(got.at[h, pl.ds(0, n_tile - 1)], send_sem.at[4 + h])
    for kind, ref in enumerate([up.at[0], down.at[1], up.at[1], down.at[0]], 6):
        settle(ref, send_sem.at[kind])


def per_device(tidal, plane_weight, plane_step, ray_angle, dest_tile, dest_segment, interp):
    n_tile = lax.axis_size("tile")
    n_depth = lax.axis_size("depth")
    rays = tidal.shape[2]
    blocks = interp.shape[1]
    lanes = blocks // n_depth
    slots = 2 * blocks // n_tile
    segments = ROWS * rays // WIDTH
    rows = segments // ROWS

    def body(*refs):
        kernel(n_depth, n_tile, *refs)

    hbm = pl.BlockSpec(memory_space=pl.ANY)
    smem = pl.BlockSpec(memory_space=pltpu.SMEM)
    vmem = pltpu.VMEM
    out = pl.pallas_call(
        body,
        out_shape=jax.ShapeDtypeStruct((rows, ROWS, WIDTH), F32),
        in_specs=[hbm, hbm, hbm, hbm, hbm, smem, smem],
        out_specs=pl.BlockSpec(memory_space=pltpu.VMEM),
        scratch_shapes=[
            vmem((3, n_depth, lanes, WIDTH), F32),
            vmem((n_depth, lanes, WIDTH), F32),
            vmem((blocks, WIDTH, WIDTH), BF16),
            vmem((1, blocks), jnp.int32),
            vmem((1, blocks), jnp.int32),
            vmem((1, WIDTH), F32),
            vmem((n_depth, 1, WIDTH), F32),
            vmem((n_depth, 3, lanes, WIDTH), F32),
            vmem((n_depth, 2 * lanes, WIDTH), F32),
            vmem((n_depth, 2 * lanes, WIDTH), F32),
            vmem((2 * blocks, WIDTH), F32),
            vmem((2 * n_tile * slots, 2 * blocks), BF16),
            vmem((n_tile, 2, blocks), F32),
            vmem((n_tile, 2, blocks), F32),
            vmem((2, n_tile, slots, WIDTH), F32),
            vmem((2, n_tile, slots, WIDTH), F32),
            vmem((segments, 2 * blocks), BF16),
            vmem((ROWS, rows, WIDTH), F32),
            vmem((ROWS, rows, WIDTH), F32),
            vmem((ROWS, rows, WIDTH), F32),
            vmem((ROWS, rows, WIDTH), F32),
            pltpu.SemaphoreType.DMA((5,)),
            pltpu.SemaphoreType.DMA((10,)),
            pltpu.SemaphoreType.DMA((10,)),
            pltpu.SemaphoreType.DMA((n_depth // X_SIZE,)),
        ],
        compiler_params=pltpu.CompilerParams(collective_id=0, vmem_limit_bytes=33554432, has_side_effects=True),
    )(
        pltpu.with_memory_space_constraint(tidal.reshape(3, n_depth, lanes, WIDTH), pltpu.HBM),
        pltpu.with_memory_space_constraint(ray_angle.reshape(n_depth, lanes, WIDTH), pltpu.HBM),
        pltpu.with_memory_space_constraint(interp[0], pltpu.HBM),
        pltpu.with_memory_space_constraint(dest_tile.reshape(1, blocks), pltpu.HBM),
        pltpu.with_memory_space_constraint(dest_segment, pltpu.HBM),
        plane_weight,
        plane_step,
    )
    return out.transpose(1, 0, 2).reshape(1, ROWS, rows * WIDTH)


def solution(mesh):
    return jax.shard_map(
        per_device,
        mesh=mesh,
        in_specs=(
            P("depth", None, "tile"),
            P("depth"),
            P("depth"),
            P("tile"),
            P("depth", "tile", None),
            P("depth", "tile"),
            P("depth", "tile", None, None),
        ),
        out_specs=P("depth", "tile", None),
        check_vma=False,
    )
```
